256 devices in a mesh: section: 2 (over core), seq: 64 (over z, y_hi, x), mp: 2 (over y_lo).
Axes of the slice: x: 4, y: 4 (y_hi: 2, y_lo: 2; y = y_hi * 2 + y_lo), z: 8, core: 2. Of those that a mesh axis runs over, the one named last changes fastest.
Arguments:
- patches: bfloat16 [32768, 1280], P(('section', 'seq')), may hold values from -6 to 6
- inner_weight: bfloat16 [3, 1280, 1280], P(None, None, 'mp'), may hold values from -0.15625 to 0.15625
- norm_gain: float32 [1280], replicated, may hold values from 0.5 to 12
- outer_weight: bfloat16 [1280, 1280], P('mp'), may hold values from -0.15625 to 0.15625
- merge_gain: float32 [1280], replicated, may hold values from 0.5 to 1.5
- windows: int32 [128, 256], P(('section', 'seq')), may hold values from 0 to 7, never falling along the last dimension, each value on 1 to 64 neighbouring positions
- owners: int32 [8192, 1], P(('section', 'seq')), may hold values from 0 to 127; in each aligned block of 64 rows (0 to 63, 64 to 127, ...) at most 2 rows name the same one
- context_query: bfloat16 [8192, 8192], P('seq', ('section', 'mp')), may hold values from -150 to 150
- context_key: bfloat16 [8192, 1024], P('seq', ('section', 'mp')), may hold values from -6 to 6
- context_value: bfloat16 [8192, 1024], P('seq', ('section', 'mp')), may hold values from -6 to 6
- documents: int32 [8192], replicated, may hold values from 0 to 7, never falling along the last dimension, each value on 1 to 6144 neighbouring positions
Outputs:
- delivered: bfloat16 [32768, 5120], P(('section', 'seq'), 'mp')
- attended: bfloat16 [8192, 8192], P('seq', ('section', 'mp'))
The draws below stay inside these ranges and needn't reach their ends.
Inputs may be any that keep to these rules, and one draw needn't show every extreme that they name: Along each row the window numbers never fall, and each of the 8 windows holds 1 to 64 patches. `owners`: among the 64 tokens of one device (aligned blocks of rows) no owner is named more than 2 times; some owner is named exactly 2 times in some blocks. Document numbers never fall; each of the 8 documents holds 1 to 6144 positions, one exactly 6144.
All inputs are finite; a program needn't handle non-finite values.
Results may differ from the reference program's by a relative error of at most 0.012.
The reference program's roundings to bfloat16 on the way count: a program that leaves them out, or rounds other values in their place, can miss the bound.
Values may be sent and summed in bfloat16 or wider, within the bound.
No kernel may reach another device: no remote copies, remote signals or barrier semaphores. Data moves between devices by JAX's collectives and lax.ppermute only.
A program may use at most 128 MiB of HBM per device.

```python
import math
import jax
import jax.numpy as jnp
import numpy as np
from jax import lax

VD = 1280
VH = 16
QH = 64
KVH = 8
HD = 128
P_DEV = 256
WIN_MOST = 64
DOCS = 8
OWNERS = 128
PATCHES = 32768
TOK_DEV = 64
MERGED = 8192
CAP = 2
WINS = 8
CONTEXT = 8192
DOC_MOST = 6144


def draw_norm_gain(key, part):
    uniform_part = jax.random.uniform(jax.random.fold_in(key, 3), (VD,), jnp.float32)
    lowest, highest = (0.5, 2.0)
    return jnp.exp(jnp.log(lowest) + uniform_part * (jnp.log(highest) - jnp.log(lowest)))


def paired_draw(key):
    query_seed = jax.random.fold_in(key, 101)
    key_seed = jax.random.fold_in(key, 102)
    key_heads = jnp.clip(jax.random.normal(key_seed, (CONTEXT, KVH, HD), jnp.float32), -5.0, 5.0)
    query_heads = jnp.clip(3.0 * jax.random.normal(query_seed, (CONTEXT, QH, HD), jnp.float32), -15.0, 15.0)
    return (query_heads.reshape(CONTEXT, QH * HD), key_heads.reshape(CONTEXT, KVH * HD))


def draw_context_query(key, part):
    return paired_draw(key)[0].astype(jnp.bfloat16)


def draw_context_key(key, part):
    return paired_draw(key)[1].astype(jnp.bfloat16)


def level_of(key, extent, split, low, high):
    level = 1.0
    for axis_at, shards_of in split:
        heights = jax.random.uniform(jax.random.fold_in(jax.random.fold_in(key, 6), axis_at), (shards_of,), jnp.float32, low / len(split), high / len(split))
        level = level * jnp.repeat(jnp.exp(heights), extent[axis_at] // shards_of).reshape((-1,) + (1,) * (len(extent) - 1 - axis_at))
    return level


def length_profile(count, total, most, slope):
    portions = [(1 << 20) // math.isqrt(grade ** slope) + 1 for grade in range(2, count + 1)]
    surplus, given = total - most - (count - 1), [1] * (count - 1)
    while surplus > 0:
        candidates = [i for i in range(count - 1) if given[i] < most]
        mass, budget = sum([portions[i] for i in candidates]), surplus
        for i in candidates:
            extra = min(most - given[i], max(1, budget * portions[i] // mass), surplus)
            given[i] = given[i] + extra
            surplus = surplus - extra
    return np.array([most] + given)


def ragged_sizes(rng, number_of, total, bound, slope):
    if number_of == 2:
        one = jax.random.randint(rng, (), max(1, total - bound), min(bound, total - 1) + 1)
        return jnp.stack([one, total - one])
    lengths = jnp.asarray(length_profile(number_of, total, bound, slope), jnp.int32)
    couples = (number_of - 1) // 2
    giver, sink = lengths[1:1 + 2 * couples:2], lengths[2:2 + 2 * couples:2]
    margin = jnp.minimum(giver - 1, bound - sink)
    shifted = jax.random.randint(jax.random.fold_in(rng, 1), (couples,), 0, 1 << 20) % (margin + 1)
    lengths = lengths.at[1:1 + 2 * couples:2].set(giver - shifted).at[2:2 + 2 * couples:2].set(sink + shifted)
    return lengths[jax.random.permutation(jax.random.fold_in(rng, 2), number_of)]


def shared_out(stream_key, own, number, rows, count, top, limit, lean):
    order = jax.random.permutation(stream_key, count)
    crowded, common = shares(count, rows * top, limit, lean, True), shares(count, rows * top, limit, lean, False)
    places = jnp.arange(count)

    def named(lengths, turn):
        used = int((lengths > 0).sum())
        fixed = max(1, used // 4)
        moved = fixed + (places - fixed + turn * (used - fixed)) % max(1, count - fixed)
        return jnp.zeros((count,), jnp.int32).at[order[jnp.where(places < fixed, places, moved)]].set(jnp.asarray(lengths, jnp.int32))

    lengths = jnp.where(number % 4 == 0, named(crowded, number // 4), named(common, number - number // 4 - 1))
    mixed = jax.random.permutation(jax.random.fold_in(own, 3), count)
    giver, taker = mixed[0:count // 2 * 2:2], mixed[1:count // 2 * 2:2]
    room = jnp.minimum(lengths[giver] - 1, limit - lengths[taker]) // 2
    room = jnp.where((giver == order[0]) | (taker == order[0]) | (lengths[taker] == 0), 0, jnp.maximum(room, 0))
    moved = jax.random.randint(jax.random.fold_in(own, 4), (count // 2,), 0, 1 << 20) % (room + 1)
    lengths = lengths.at[giver].add(-moved).at[taker].add(moved)
    members = jnp.searchsorted(jnp.cumsum(lengths), jnp.arange(rows * top), side="right").astype(jnp.int32)
    table = members.reshape(top, rows).T
    table = table[jax.random.permutation(jax.random.fold_in(own, 1), rows)]
    turn = jax.random.randint(jax.random.fold_in(own, 2), (rows, 1), 0, top)
    return jnp.take_along_axis(table, (jnp.arange(top)[None, :] + turn) % top, axis=1)


def shares(count, total, reach, lean, full):
    portions = [(1 << 20) // math.isqrt(grade ** lean) + 1 for grade in range(1, count + 1)]
    largest = reach if full else min(reach, max(-(-total // count), total * portions[0] // sum(portions)))
    least = 1 if total - largest >= count - 1 else 0
    holding, spare = [largest] + [least] * (count - 1), total - largest - least * (count - 1)
    while spare > 0:
        candidates = [i for i in range(1, count) if holding[i] < largest] or [i for i in range(1, count) if holding[i] < reach]
        whole, remaining = sum([portions[i] for i in candidates]), spare
        for i in candidates:
            more = min(reach - holding[i], max(1, remaining * portions[i] // whole), spare)
            holding[i] = holding[i] + more
            spare = spare - more
    return np.array(holding)


def scatter_about(stream_key, shape, width, most, cuts=(), kind=jnp.bfloat16):
    result = jax.random.normal(stream_key, shape, jnp.float32) * width
    if len(cuts) > 0:
        result = level_of(stream_key, shape, cuts, -0.22, 0.18) * result
    return jnp.clip(result, min=-most, max=most).astype(kind)


def setup_inputs(seed: int = 0) -> dict:
    streams_of = jax.random.split(jax.random.key(seed), 12)
    patches = scatter_about(streams_of[0], (PATCHES, VD), 1.0, 6.0, ((0, 128),))
    inner_weight = scatter_about(streams_of[1], (3, VD, VD), VD ** -0.5, 0.15625, ((2, 2),))
    norm_gain = draw_norm_gain(jax.random.fold_in(streams_of[11], 71), 0)
    outer_weight = scatter_about(streams_of[3], (VD, VD), VD ** -0.5, 0.15625, ((0, 2),))
    merge_gain = jnp.clip(1.0 + 0.1 * jax.random.normal(streams_of[4], (VD,), jnp.float32), 0.5, 1.5)
    windows = jax.vmap(lambda own: jnp.searchsorted(jnp.cumsum(ragged_sizes(own, WINS, P_DEV, WIN_MOST, 0)), jnp.arange(P_DEV), side="right"))(jax.random.split(streams_of[5], OWNERS)).reshape((OWNERS, P_DEV)).astype(jnp.int32)
    owners_keys = jax.random.split(jax.random.fold_in(streams_of[6], 1), MERGED // TOK_DEV)
    owners_turns = jax.random.permutation(jax.random.fold_in(streams_of[6], 3), MERGED // TOK_DEV)
    owners = jax.vmap(lambda own, number: shared_out(jax.random.fold_in(streams_of[6], 2), own, number, TOK_DEV, OWNERS, 1, CAP, 2))(owners_keys, owners_turns).reshape((MERGED, 1))
    context_query = draw_context_query(jax.random.fold_in(streams_of[11], 71), 0)
    context_key = draw_context_key(jax.random.fold_in(streams_of[11], 71), 0)
    context_value = scatter_about(streams_of[9], (CONTEXT, KVH * HD), 1.0, 6.0, ((0, 64), (1, 4)))
    documents = jnp.searchsorted(jnp.cumsum(ragged_sizes(streams_of[10], DOCS, CONTEXT, DOC_MOST, 1)), jnp.arange(CONTEXT), side="right").astype(jnp.int32)
    return {"patches": patches, "inner_weight": inner_weight, "norm_gain": norm_gain, "outer_weight": outer_weight, "merge_gain": merge_gain, "windows": windows, "owners": owners, "context_query": context_query, "context_key": context_key, "context_value": context_value, "documents": documents}


EPSILON = 1e-06

def rms_scale(values, gain):
    return values * lax.rsqrt(lax.optimization_barrier(jnp.mean(values * values, axis=-1, keepdims=True)) + EPSILON) * gain

def settle(values):
    return lax.optimization_barrier(values.astype(jnp.bfloat16)).astype(jnp.float32)

def vision_merge(patches, inner_weight, norm_gain, outer_weight, merge_gain, windows):
    head_dim = VD // VH

    def one_block(inputs):
        patch_block, window_row = inputs
        source = patch_block.astype(jnp.float32)
        normed = rms_scale(source, norm_gain).astype(jnp.bfloat16)
        query_heads = settle(jnp.dot(normed, inner_weight[0], preferred_element_type=jnp.float32)).reshape(P_DEV, VH, head_dim)
        key_heads = settle(jnp.dot(normed, inner_weight[1], preferred_element_type=jnp.float32)).reshape(P_DEV, VH, head_dim)
        value_heads = settle(jnp.dot(normed, inner_weight[2], preferred_element_type=jnp.float32)).reshape(P_DEV, VH, head_dim)
        scores = jnp.einsum('qhd,khd->hqk', query_heads, key_heads) / math.sqrt(head_dim)
        allowed = window_row[:, None] == window_row[None, :]
        scores = jnp.where(allowed[None], scores, -jnp.inf)
        row_peak = lax.optimization_barrier(jnp.max(scores, axis=-1, keepdims=True))
        weights = jnp.exp(scores - row_peak)
        denominator = lax.optimization_barrier(jnp.sum(weights, axis=-1))
        context = jnp.einsum('hqk,khd->qhd', settle(weights), value_heads)
        context = (context / jnp.transpose(denominator)[:, :, None]).astype(jnp.bfloat16).reshape(P_DEV, VD)
        residual = source + jnp.dot(context, outer_weight, preferred_element_type=jnp.float32)
        merged = rms_scale(residual, merge_gain).astype(jnp.bfloat16)
        return merged.reshape(P_DEV // 4, 4 * VD)
    blocks = lax.map(one_block, (patches.reshape(OWNERS, P_DEV, VD), windows))
    return blocks.reshape(MERGED, 4 * VD)

def place_tokens(merged, owners):
    target = owners[:, 0].reshape(OWNERS, TOK_DEV)
    order = jnp.arange(TOK_DEV, dtype=jnp.int32)
    earlier = order[None, :] < order[:, None]
    slot_rank = lax.optimization_barrier(jnp.sum((target[:, :, None] == target[:, None, :]) & earlier[None], axis=2)).astype(jnp.int32)
    source_block = jnp.arange(OWNERS, dtype=jnp.int32)[:, None]
    destination = ((target * OWNERS + source_block) * CAP + slot_rank).reshape(MERGED).astype(jnp.int32)
    empty = jnp.zeros((OWNERS * OWNERS * CAP, 4 * VD), jnp.bfloat16)
    return empty.at[destination].set(merged)

def context_attention(context_query, context_key, context_value, documents):
    groups = QH // KVH
    key_heads = context_key.astype(jnp.float32).reshape(CONTEXT, KVH, HD)
    value_heads = context_value.astype(jnp.float32).reshape(CONTEXT, KVH, HD)
    positions = jnp.arange(CONTEXT, dtype=jnp.int32)
    query_block = math.gcd(CONTEXT, 256)

    def one_block(offset):
        query_heads = lax.dynamic_slice_in_dim(context_query, offset, query_block, 0).astype(jnp.float32)
        query_heads = query_heads.reshape(query_block, KVH, groups, HD)
        scores = jnp.einsum('qhgd,khd->hgqk', query_heads, key_heads) / math.sqrt(HD)
        query_positions = offset + jnp.arange(query_block, dtype=jnp.int32)
        query_docs = lax.dynamic_slice_in_dim(documents, offset, query_block, 0)
        allowed = (positions[None, :] <= query_positions[:, None]) & (documents[None, :] == query_docs[:, None])
        scores = jnp.where(allowed[None, None], scores, -jnp.inf)
        row_peak = lax.optimization_barrier(jnp.max(scores, axis=-1, keepdims=True))
        weights = jnp.exp(scores - row_peak)
        denominator = lax.optimization_barrier(jnp.sum(weights, axis=-1))
        output = jnp.einsum('hgqk,khd->qhgd', settle(weights), value_heads)
        output = output / jnp.transpose(denominator, (2, 0, 1))[..., None]
        return output.astype(jnp.bfloat16).reshape(query_block, QH * HD)
    starts = (jnp.arange(CONTEXT // query_block, dtype=jnp.int32) * query_block).astype(jnp.int32)
    return lax.map(one_block, starts).reshape(CONTEXT, QH * HD)

def reference(patches, inner_weight, norm_gain, outer_weight, merge_gain, windows, owners, context_query, context_key, context_value, documents):
    merged = vision_merge(patches, inner_weight, norm_gain, outer_weight, merge_gain, windows)
    delivered = place_tokens(merged, owners)
    attended = context_attention(context_query, context_key, context_value, documents)
    return (delivered, attended)
```

```python
import math

import jax
import jax.numpy as jnp
from jax import lax
from jax.experimental import pallas as pl
from jax.experimental.pallas import tpu as pltpu
from jax.sharding import PartitionSpec as P


HD = 128
EPSILON = 1e-06
BOTH = ("section", "seq")
BF = jnp.bfloat16
F32 = jnp.float32
NZ, NY, NX = 8, 2, 4
QUAD = 512
NT = (((1,), (1,)), ((), ()))


def vision_kernel(m_ref, x_ref, w_hbm, gain_ref, ow_hbm, win_ref, send_ref, keep_ref,
                  w_buf, ow_buf, ctx_ref, part_ref, xp_ref, sems):
    copies = [pltpu.make_async_copy(w_hbm.at[i], w_buf.at[i], sems.at[i]) for i in range(3)]
    copies.append(pltpu.make_async_copy(ow_hbm, ow_buf, sems.at[3]))
    for c in copies:
        c.start()
    rows = x_ref.shape[0]
    i = lax.broadcasted_iota(jnp.int32, (rows, rows), 0)
    j = lax.broadcasted_iota(jnp.int32, (rows, rows), 1)
    tokens = rows // 4
    perm = jnp.where(j == 4 * (i & (tokens - 1)) + i // tokens, 1.0, 0.0).astype(BF)
    xp = jnp.dot(perm, x_ref[...], preferred_element_type=F32)
    xp_ref[...] = xp
    scale = lax.rsqrt(jnp.mean(xp * xp, axis=-1, keepdims=True) + EPSILON)
    normed = (xp * scale * gain_ref[...]).astype(BF)
    win = jnp.broadcast_to(win_ref[...], (128, rows)).astype(F32).astype(BF)
    win_row = lax.dot_general(win, perm, NT, preferred_element_type=F32)[0:1]
    win_col = lax.dot_general(perm, win, NT, preferred_element_type=F32)[:, 0:1]
    allowed = win_row == win_col
    heads = []
    for n in range(3):
        copies[n].wait()
        heads.append(jnp.dot(normed, w_buf[n], preferred_element_type=F32).astype(BF))
    q, k, v = heads
    hd = 80
    local = q.shape[1] // hd
    for h in range(local):
        lo, hi = h * hd, (h + 1) * hd
        a, b = lo // 128 * 128, -(-hi // 128) * 128
        col = lax.broadcasted_iota(jnp.int32, (rows, b - a), 1) + a
        mine = (col >= lo) & (col < hi)
        qh = jnp.where(mine, q[:, a:b].astype(F32), 0.0).astype(BF)
        s = lax.dot_general(qh, k[:, a:b], NT, preferred_element_type=F32) * (1.0 / math.sqrt(hd))
        s = jnp.where(allowed, s, -1e30)
        p = jnp.exp(s - jnp.max(s, axis=-1, keepdims=True))
        den = jnp.sum(p, axis=-1, keepdims=True)
        o = jnp.dot(p.astype(BF), v[:, a:b], preferred_element_type=F32) / den
        if lo == a:
            ctx_ref[:, a:b] = o
        else:
            ctx_ref[:, a:b] = jnp.where(mine, o, ctx_ref[:, a:b] if b - a == 128 else
                                        jnp.concatenate([ctx_ref[:, a:a + 128], o[:, 128:]], axis=1))
    copies[3].wait()
    part_ref[...] = jnp.dot(ctx_ref[...].astype(BF), ow_buf[...], preferred_element_type=F32)
    half = rows // 2
    m = m_ref[0]
    own = pl.multiple_of(m * half, half)
    other = pl.multiple_of((1 - m) * half, half)
    send_ref[...] = part_ref[pl.ds(other, half), :].astype(BF)
    keep_ref[...] = part_ref[pl.ds(own, half), :] + xp_ref[pl.ds(own, half), :]


def vision(m, patches, inner_weight, norm_gain, outer_weight, windows):
    rows, vd = patches.shape
    cols = inner_weight.shape[2]
    vm = pl.BlockSpec(memory_space=pltpu.VMEM)
    hbm = pl.BlockSpec(memory_space=pl.ANY)
    return pl.pallas_call(
        vision_kernel,
        in_specs=[pl.BlockSpec(memory_space=pltpu.SMEM), vm, hbm, vm, hbm, vm],
        out_specs=[vm, vm],
        out_shape=[jax.ShapeDtypeStruct((rows // 2, vd), BF), jax.ShapeDtypeStruct((rows // 2, vd), F32)],
        scratch_shapes=[
            pltpu.VMEM((3, vd, cols), BF),
            pltpu.VMEM((cols, vd), BF),
            pltpu.VMEM((rows, cols), F32),
            pltpu.VMEM((rows, vd), F32),
            pltpu.VMEM((rows, vd), F32),
            pltpu.SemaphoreType.DMA((4,)),
        ],
        cost_estimate=pl.CostEstimate(flops=3 * 10**9, bytes_accessed=8 * 10**6, transcendentals=10**6),
        name="vision",
    )(m, patches, inner_weight, norm_gain.reshape(1, vd), outer_weight, windows)


def merge_kernel(keep_ref, recv_ref, gain_ref, target_ref, out_ref):
    r = keep_ref[...] + recv_ref[...].astype(F32)
    merged = (r * lax.rsqrt(jnp.mean(r * r, axis=-1, keepdims=True) + EPSILON) * gain_ref[...]).astype(BF)
    half = r.shape[0] // 2
    w = r.shape[1] // 2
    quarters = jnp.concatenate(
        [merged[:half, :w], merged[:half, w:], merged[half:, :w], merged[half:, w:]], axis=0)
    n = out_ref.shape[0]
    step = 256
    for b in range(n // step):
        i = lax.broadcasted_iota(jnp.int32, (step, 4 * half), 0) + b * step
        place = jnp.where(target_ref[...] == i, 1.0, 0.0).astype(BF)
        out_ref[b * step:(b + 1) * step, :] = jnp.dot(
            place, quarters, preferred_element_type=F32).astype(BF)


def merge(keep, recv, merge_gain, target, slots):
    vm = pl.BlockSpec(memory_space=pltpu.VMEM)
    return pl.pallas_call(
        merge_kernel,
        in_specs=[vm] * 4,
        out_specs=vm,
        out_shape=jax.ShapeDtypeStruct((slots * 4, keep.shape[1] // 2), BF),
        cost_estimate=pl.CostEstimate(flops=4 * 10**8, bytes_accessed=3 * 10**6, transcendentals=10**4),
        name="merge",
    )(keep, recv, merge_gain.reshape(1, -1), target)


def place_kernel(in_ref, out_ref):
    n, w = in_ref.shape
    i = lax.broadcasted_iota(jnp.int32, (n, n), 0)
    j = lax.broadcasted_iota(jnp.int32, (n, n), 1)
    quarter = n // 4
    perm = jnp.where(j == 4 * (i & (quarter - 1)) + i // quarter, 1.0, 0.0).astype(BF)
    y = jnp.dot(perm, in_ref[...], preferred_element_type=F32).astype(BF)
    for q in range(4):
        out_ref[:, q * w:(q + 1) * w] = y[q * quarter:(q + 1) * quarter]


def place(arrived):
    n, w = arrived.shape
    step = 256
    return pl.pallas_call(
        place_kernel,
        grid=(n // step,),
        in_specs=[pl.BlockSpec((step, w), lambda i: (i, 0))],
        out_specs=pl.BlockSpec((step // 4, 4 * w), lambda i: (i, 0)),
        out_shape=jax.ShapeDtypeStruct((n // 4, 4 * w), BF),
        cost_estimate=pl.CostEstimate(flops=4 * 10**8, bytes_accessed=3 * 10**6, transcendentals=0),
        name="place",
    )(arrived)


def perm_of(move):
    pairs = []
    for c in range(2):
        for z in range(NZ):
            for y in range(NY):
                for x in range(NX):
                    a, b, d, e = move(c, z, y, x)
                    pairs.append((((c * NZ + z) * NY + y) * NX + x, ((a * NZ + b) * NY + d) * NX + e))
    return pairs


def quad_move(p):
    return perm_of(lambda c, z, y, x: (z >> 1 & 1, 2 * (2 * c + (p ^ z >> 2)) + (z & 1), y, x))


def attend_kernel(meta_ref, q_ref, *rest):
    near, far = rest[:4], rest[4:8]
    starts_ref, ends_ref, o_ref, q_scr, m_scr, acc_scr = rest[8:]
    x, c, here, first = [meta_ref[n] for n in range(4)]
    chips = [x, (x + 3) & 3, (x + 1) & 3, (x + 2) & 3]
    starts, ends = starts_ref[...], ends_ref[...]
    chain = q_scr.shape[0] // 2

    def same_doc(base, n):
        at = lax.broadcasted_iota(jnp.int32, (n, HD), 0) + base
        return (at >= starts) & (at < ends)

    other = jnp.where(same_doc(here * QUAD + x * 128, 128), 0.0, -1e30).astype(BF)
    for g in range(8):
        q_scr[g * 128:(g + 1) * 128, :HD] = other
        q_scr[g * 128:(g + 1) * 128, HD:] = q_ref[:, g * 128:(g + 1) * 128]
    factor = math.log2(math.e) / math.sqrt(HD)

    def keys_of(b):
        at, hi = (b ^ here) & 3, b >> 3
        own = (b >> 2 & 1) == c
        kv = jnp.concatenate(
            [jnp.where(own, n[at, hi], f[at, hi]) for n, f in zip(near, far)], axis=0)
        same = jnp.concatenate(
            [jnp.where(same_doc(b * QUAD + t * 128, 128), 1.0, 0.0) for t in chips], axis=0).astype(BF)
        return (jnp.concatenate([same, kv[:, :HD]], axis=1),
                jnp.concatenate([kv[:, HD:], jnp.ones((QUAD, HD), BF)], axis=1))

    i = lax.broadcasted_iota(jnp.int32, (chain, QUAD), 0)
    j = lax.broadcasted_iota(jnp.int32, (chain, QUAD), 1)
    ahead = jnp.where(j < 128, x, jnp.where(j < 256, chips[1], jnp.where(j < 384, chips[2], chips[3])))
    causal = ahead * 128 + (j & 127) <= x * 128 + (i & 127)
    keys, values = keys_of(here)
    for g in range(2):
        part = pl.ds(g * chain, chain)
        s = lax.dot_general(q_scr[part], keys, NT, preferred_element_type=F32)
        s = jnp.where(causal, s, -1e30)
        new = jnp.broadcast_to(jnp.max(s, axis=-1, keepdims=True), (chain, HD))
        m_scr[part] = new
        w = jnp.exp2((s - jnp.tile(new, (1, QUAD // HD))) * factor)
        acc_scr[part] = jnp.dot(w.astype(BF), values, preferred_element_type=F32)

    @pl.loop(first, here)
    def _(b):
        keys, values = keys_of(b)
        for g in range(2):
            part = pl.ds(g * chain, chain)
            s = lax.dot_general(q_scr[part], keys, NT, preferred_element_type=F32)
            old = m_scr[part]
            new = jnp.maximum(old, jnp.max(s, axis=-1, keepdims=True))
            m_scr[part] = new
            w = jnp.exp2((s - jnp.tile(new, (1, QUAD // HD))) * factor)
            alpha = jnp.exp2((old - new) * factor)
            acc_scr[part] = acc_scr[part] * jnp.tile(alpha, (1, 2)) + jnp.dot(
                w.astype(BF), values, preferred_element_type=F32)

    for g in range(8):
        part = pl.ds(g * 128, 128)
        o_ref[:, g * 128:(g + 1) * 128] = (acc_scr[part, :HD] / acc_scr[part, HD:]).astype(BF)


def attend(meta, query, near, far, starts, ends):
    pieces = [*near, *far]
    vm = pl.BlockSpec(memory_space=pltpu.VMEM)
    return pl.pallas_call(
        attend_kernel,
        in_specs=[pl.BlockSpec(memory_space=pltpu.SMEM)] + [vm] * 11,
        out_specs=vm,
        out_shape=jax.ShapeDtypeStruct((128, 1024), BF),
        scratch_shapes=[
            pltpu.VMEM((1024, 2 * HD), BF),
            pltpu.VMEM((1024, HD), F32),
            pltpu.VMEM((1024, 2 * HD), F32),
        ],
        compiler_params=pltpu.CompilerParams(vmem_limit_bytes=32 << 20),
        cost_estimate=pl.CostEstimate(flops=4 * 10**9, bytes_accessed=3 * 10**6, transcendentals=5 * 10**6),
        name="attend",
    )(meta, query, *pieces, starts, ends)


def pack_kernel(*refs):
    for n, ref in enumerate(refs[:-1]):
        refs[-1][n] = ref[...]


def pack(parts):
    vm = pl.BlockSpec(memory_space=pltpu.VMEM)
    return pl.pallas_call(
        pack_kernel,
        in_specs=[vm] * len(parts),
        out_specs=vm,
        out_shape=jax.ShapeDtypeStruct((len(parts),) + parts[0].shape, BF),
        cost_estimate=pl.CostEstimate(flops=0, bytes_accessed=10**6, transcendentals=0),
        name="pack",
    )(*parts)


def context_part(context_query, context_key, context_value, documents):
    c = lax.axis_index("section")
    s = lax.axis_index("seq")
    z, y, x = s // (NX * NY), (s // NX) % NY, s % NX
    a, par = z // 2, z & 1
    odd, hi = a & 1, a >> 1
    head = [
        jnp.concatenate([t[:, j * HD:(j + 1) * HD] for t in (context_key, context_value)], axis=1)
        for j in range(2)
    ]
    got = []
    for p in range(2):
        got.append(lax.ppermute(jnp.where((hi ^ p) == 0, head[0], head[1]), BOTH, quad_move(p)))
    mine = jnp.where(odd == 0, jnp.stack(got), jnp.stack(got[::-1]))
    parts = [mine]
    for d, e in ((0, 1), (1, 0), (1, 1)):
        parts.append(lax.ppermute(mine, "seq", [(t, t ^ (8 * d + 4 * e)) for t in range(64)]))
    near = [pack(parts)]
    for step in (1, -1, 2):
        near.append(lax.ppermute(near[0], "seq", [(t, t // 4 * 4 + (t + step) % 4) for t in range(64)]))
    far = []
    for n in range(4):
        far.append(lax.ppermute(near[n], "section", [(0, 1), (1, 0)]))
    queries = []
    for p in range(2):
        queries.append(lax.ppermute(
            jnp.where((hi ^ p) == 0, context_query[:, :1024], context_query[:, 1024:]),
            BOTH, quad_move(p)))
    place = [(2 * (p ^ odd) + c) * 2048 + (s & 15) * 128 for p in range(2)]
    row_docs = jnp.stack([lax.dynamic_slice_in_dim(documents, t, 1, 0)[0] for t in place])
    firsts = jnp.sum(documents[None, :] < row_docs[:, None], axis=1).astype(jnp.int32) // QUAD
    names = jnp.arange(8, dtype=jnp.int32)
    pad = jnp.full((HD - 8,), 8192, jnp.int32)
    starts = jnp.sum(documents[None, :] < names[:, None], axis=1).astype(jnp.int32)
    ends = jnp.sum(documents[None, :] <= names[:, None], axis=1).astype(jnp.int32)
    starts = jnp.concatenate([starts, pad]).reshape(1, HD)
    ends = jnp.concatenate([ends, pad]).reshape(1, HD)
    back = []
    for p in range(2):
        meta = jnp.stack([x, c, (2 * (p ^ odd) + c) * 4 + par * 2 + y, firsts[p]]).astype(jnp.int32)
        o = attend(meta, queries[p], near, far, starts, ends)
        back.append(lax.ppermute(o, BOTH, [(t, f) for f, t in quad_move(p)]))
    return jnp.where(hi == 0, jnp.concatenate(back, axis=1), jnp.concatenate(back[::-1], axis=1))


def program(
    patches,
    inner_weight,
    norm_gain,
    outer_weight,
    merge_gain,
    windows,
    owners,
    context_query,
    context_key,
    context_value,
    documents,
):
    m = lax.axis_index("mp").astype(jnp.int32).reshape(1)
    send, keep = vision(m, patches, inner_weight, norm_gain, outer_weight, windows)
    recv = lax.ppermute(send, "mp", [(0, 1), (1, 0)])
    tokens = owners.shape[0]
    target = owners[:, 0]
    order = jnp.arange(tokens, dtype=jnp.int32)
    earlier = (target[:, None] == target[None, :]) & (order[:, None] < order[None, :])
    slot = target * 2 + jnp.sum(earlier, axis=0).astype(jnp.int32)
    spot = (4 * slot[None, :] + jnp.arange(4, dtype=jnp.int32)[:, None]).reshape(1, 4 * tokens)
    owner_count = lax.axis_size(BOTH)
    outgoing = merge(keep, recv, merge_gain, spot, owner_count * 2)
    arrived = lax.all_to_all(
        outgoing.reshape(owner_count, 8, outgoing.shape[1]), BOTH, split_axis=0, concat_axis=0, tiled=True)
    delivered = place(arrived.reshape(outgoing.shape))
    attended = context_part(context_query, context_key, context_value, documents)
    return (delivered, attended)


def solution(mesh):
    in_specs = (
        P(BOTH, None),
        P(None, None, "mp"),
        P(),
        P("mp", None),
        P(),
        P(BOTH, None),
        P(BOTH, None),
        P("seq", ("section", "mp")),
        P("seq", ("section", "mp")),
        P("seq", ("section", "mp")),
        P(),
    )
    out_specs = (P(BOTH, "mp"), P("seq", ("section", "mp")))
    return jax.shard_map(program, mesh=mesh, in_specs=in_specs, out_specs=out_specs, check_vma=False)
```

```python
import functools
import math

import jax
import jax.numpy as jnp
from jax import lax
from jax.experimental import pallas as pl
from jax.experimental.pallas import tpu as pltpu
from jax.sharding import PartitionSpec as P


HD = 128
EPSILON = 1e-06
BOTH = ("section", "seq")
BF = jnp.bfloat16
F32 = jnp.float32
NZ, NY, NX = 8, 2, 4
QUAD = 512
NT = (((1,), (1,)), ((), ()))


def row_of(ref):
    return jnp.concatenate([ref[n:n + 1] for n in range(ref.shape[0])], axis=1)


def vision_kernel(x_ref, w_hbm, gain_ref, ow_hbm, win_ref, send_ref, keep_ref,
                  w_ref, ow_ref, ctx_ref, part_ref, xp_ref, sems):
    copies = [pltpu.make_async_copy(w_hbm.at[i], w_ref.at[i], sems.at[i]) for i in range(3)]
    copies.append(pltpu.make_async_copy(ow_hbm, ow_ref, sems.at[3]))
    for c in copies:
        c.start()
    rows = x_ref.shape[0]
    i = lax.broadcasted_iota(jnp.int32, (rows, rows), 0)
    j = lax.broadcasted_iota(jnp.int32, (rows, rows), 1)
    tokens = rows // 4
    perm = jnp.where(j == 4 * (i & (tokens - 1)) + i // tokens, 1.0, 0.0).astype(BF)
    xp = jnp.dot(perm, x_ref[...], preferred_element_type=F32)
    xp_ref[...] = xp
    scale = lax.rsqrt(jnp.mean(xp * xp, axis=-1, keepdims=True) + EPSILON)
    normed = (xp * scale * row_of(gain_ref)).astype(BF)
    win = jnp.broadcast_to(win_ref[...], (128, rows)).astype(F32).astype(BF)
    win_row = lax.dot_general(win, perm, NT, preferred_element_type=F32)[0:1]
    win_col = lax.dot_general(perm, win, NT, preferred_element_type=F32)[:, 0:1]
    allowed = win_row == win_col
    heads = []
    for n in range(3):
        copies[n].wait()
        heads.append(jnp.dot(normed, w_ref[n], preferred_element_type=F32).astype(BF))
    q, k, v = heads
    hd = 80
    local = q.shape[1] // hd
    for h in range(local):
        lo, hi = h * hd, (h + 1) * hd
        a, b = lo // 128 * 128, -(-hi // 128) * 128
        col = lax.broadcasted_iota(jnp.int32, (rows, b - a), 1) + a
        mine = (col >= lo) & (col < hi)
        qh = jnp.where(mine, q[:, a:b].astype(F32), 0.0).astype(BF)
        s = lax.dot_general(qh, k[:, a:b], NT, preferred_element_type=F32) * (1.0 / math.sqrt(hd))
        s = jnp.where(allowed, s, -1e30)
        p = jnp.exp(s - jnp.max(s, axis=-1, keepdims=True))
        den = jnp.sum(p, axis=-1, keepdims=True)
        o = jnp.dot(p.astype(BF), v[:, a:b], preferred_element_type=F32) / den
        if lo == a:
            ctx_ref[:, a:b] = o
        else:
            ctx_ref[:, a:b] = jnp.where(mine, o, ctx_ref[:, a:b] if b - a == 128 else
                                        jnp.concatenate([ctx_ref[:, a:a + 128], o[:, 128:]], axis=1))
    copies[3].wait()
    part_ref[...] = jnp.dot(ctx_ref[...].astype(BF), ow_ref[...], preferred_element_type=F32)
    half = rows // 2
    m = lax.axis_index("mp")
    own = pl.multiple_of(m * half, half)
    other = pl.multiple_of((1 - m) * half, half)
    send_ref[...] = part_ref[pl.ds(other, half), :].astype(BF)
    keep_ref[...] = part_ref[pl.ds(own, half), :] + xp_ref[pl.ds(own, half), :]


def vision(patches, inner_weight, norm_gain, outer_weight, windows):
    rows, vd = patches.shape
    cols = inner_weight.shape[2]
    vm = pl.BlockSpec(memory_space=pltpu.VMEM)
    hbm = pl.BlockSpec(memory_space=pl.ANY)
    return pl.pallas_call(
        vision_kernel,
        in_specs=[vm, hbm, vm, hbm, vm],
        out_specs=[vm, vm],
        out_shape=[jax.ShapeDtypeStruct((rows // 2, vd), BF), jax.ShapeDtypeStruct((rows // 2, vd), F32)],
        scratch_shapes=[
            pltpu.VMEM((3, vd, cols), BF),
            pltpu.VMEM((cols, vd), BF),
            pltpu.VMEM((rows, cols), F32),
            pltpu.VMEM((rows, vd), F32),
            pltpu.VMEM((rows, vd), F32),
            pltpu.SemaphoreType.DMA((4,)),
        ],
        cost_estimate=pl.CostEstimate(flops=3 * 10**9, bytes_accessed=8 * 10**6, transcendentals=10**6),
        name="vision",
    )(patches, inner_weight, norm_gain.reshape(-1, 128), outer_weight, windows)


def merge_kernel(keep_ref, recv_ref, gain_ref, target_ref, out_ref):
    r = keep_ref[...] + recv_ref[...].astype(F32)
    merged = (r * lax.rsqrt(jnp.mean(r * r, axis=-1, keepdims=True) + EPSILON) * row_of(gain_ref)).astype(BF)
    half = r.shape[0] // 2
    w = r.shape[1] // 2
    quarters = jnp.concatenate(
        [merged[:half, :w], merged[:half, w:], merged[half:, :w], merged[half:, w:]], axis=0)
    n = out_ref.shape[0]
    step = 256
    for b in range(n // step):
        i = lax.broadcasted_iota(jnp.int32, (step, 4 * half), 0) + b * step
        place = jnp.where(target_ref[...] == i, 1.0, 0.0).astype(BF)
        out_ref[b * step:(b + 1) * step, :] = jnp.dot(
            place, quarters, preferred_element_type=F32).astype(BF)


def merge(keep, recv, merge_gain, target, slots):
    vm = pl.BlockSpec(memory_space=pltpu.VMEM)
    return pl.pallas_call(
        merge_kernel,
        in_specs=[vm] * 4,
        out_specs=vm,
        out_shape=jax.ShapeDtypeStruct((slots * 4, keep.shape[1] // 2), BF),
        compiler_params=pltpu.CompilerParams(vmem_limit_bytes=12 << 20),
        cost_estimate=pl.CostEstimate(flops=4 * 10**8, bytes_accessed=3 * 10**6, transcendentals=10**4),
        name="merge",
    )(keep, recv, merge_gain.reshape(-1, 128), target)


def place_kernel(in_ref, out_ref):
    n, w = 128, in_ref.shape[1]
    i = lax.broadcasted_iota(jnp.int32, (n, n), 0)
    j = lax.broadcasted_iota(jnp.int32, (n, n), 1)
    quarter = n // 4
    perm = jnp.where(j == 4 * (i & (quarter - 1)) + i // quarter, 1.0, 0.0).astype(BF)
    for b in range(in_ref.shape[0] // n):
        y = jnp.dot(perm, in_ref[b * n:(b + 1) * n], preferred_element_type=F32).astype(BF)
        for q in range(4):
            out_ref[b * quarter:(b + 1) * quarter, q * w:(q + 1) * w] = y[q * quarter:(q + 1) * quarter]


def place(arrived):
    n, w = arrived.shape
    step = 512
    return pl.pallas_call(
        place_kernel,
        grid=(n // step,),
        in_specs=[pl.BlockSpec((step, w), lambda i: (i, 0))],
        out_specs=pl.BlockSpec((step // 4, 4 * w), lambda i: (i, 0)),
        out_shape=jax.ShapeDtypeStruct((n // 4, 4 * w), BF),
        compiler_params=pltpu.CompilerParams(vmem_limit_bytes=12 << 20),
        cost_estimate=pl.CostEstimate(flops=4 * 10**8, bytes_accessed=3 * 10**6, transcendentals=0),
        name="place",
    )(arrived)


def perm_of(move):
    pairs = []
    for c in range(2):
        for z in range(NZ):
            for y in range(NY):
                for x in range(NX):
                    a, b, d, e = move(c, z, y, x)
                    pairs.append((((c * NZ + z) * NY + y) * NX + x, ((a * NZ + b) * NY + d) * NX + e))
    return pairs


def quad_move(p):
    return perm_of(lambda c, z, y, x: (z >> 1 & 1, 2 * (2 * c + (p ^ z >> 2)) + (z & 1), y, x))


def attend_kernel(p, bound_ref, q_ref, *rest):
    near, far = rest[:4], rest[4:8]
    o_ref, q_scr, m_scr, acc_scr = rest[8:]
    c, s = lax.axis_index("section"), lax.axis_index("seq")
    x = s & 3
    here = (2 * (p ^ (s >> 4 & 1)) + c) * 4 + (s >> 2 & 3)
    bounds = [bound_ref[n] for n in range(9)]
    begin = jnp.int32(0)
    for b in bounds[:8]:
        begin = jnp.where(b <= here * QUAD + x * 128, b, begin)
    first = begin // QUAD
    lane = lax.broadcasted_iota(jnp.int32, (1, HD), 1)
    starts = ends = jnp.full((1, HD), 16 * QUAD, jnp.int32)
    for n in range(8):
        starts = jnp.where(lane == n, bounds[n], starts)
        ends = jnp.where(lane == n, bounds[n + 1], ends)
    chips = [x, (x + 3) & 3, (x + 1) & 3, (x + 2) & 3]
    chain = q_scr.shape[0] // 4

    def same_doc(base, n):
        at = lax.broadcasted_iota(jnp.int32, (n, HD), 0) + base
        return (at >= starts) & (at < ends)

    other = jnp.where(same_doc(here * QUAD + x * 128, 128), 0.0, -1e30).astype(BF)
    for g in range(8):
        q_scr[g * 128:(g + 1) * 128, :HD] = other
        q_scr[g * 128:(g + 1) * 128, HD:] = q_ref[:, g * 128:(g + 1) * 128]
    factor = math.log2(math.e) / math.sqrt(HD)

    def keys_of(b):
        at, hi = (b ^ here) & 3, b >> 3
        own = (b >> 2 & 1) == c
        kv = jnp.concatenate(
            [jnp.where(own, n[at, hi], f[at, hi]) for n, f in zip(near, far)], axis=0)
        same = jnp.concatenate(
            [jnp.where(same_doc(b * QUAD + t * 128, 128), 1.0, 0.0) for t in chips], axis=0).astype(BF)
        return (jnp.concatenate([same, kv[:, :HD]], axis=1),
                jnp.concatenate([kv[:, HD:], jnp.ones((QUAD, HD), BF)], axis=1))

    i = lax.broadcasted_iota(jnp.int32, (chain, QUAD), 0)
    j = lax.broadcasted_iota(jnp.int32, (chain, QUAD), 1)
    ahead = jnp.where(j < 128, x, jnp.where(j < 256, chips[1], jnp.where(j < 384, chips[2], chips[3])))
    causal = ahead * 128 + (j & 127) <= x * 128 + (i & 127)
    keys, values = keys_of(here)
    for g in range(4):
        part = pl.ds(g * chain, chain)
        s = lax.dot_general(q_scr[part], keys, NT, preferred_element_type=F32)
        s = jnp.where(causal, s, -1e30)
        new = jnp.broadcast_to(jnp.max(s, axis=-1, keepdims=True), (chain, HD))
        m_scr[part] = new
        w = jnp.exp2((s - jnp.tile(new, (1, QUAD // HD))) * factor)
        acc_scr[part] = jnp.dot(w.astype(BF), values, preferred_element_type=F32)

    @pl.loop(first, here)
    def _(b):
        keys, values = keys_of(b)
        for g in range(4):
            part = pl.ds(g * chain, chain)
            s = lax.dot_general(q_scr[part], keys, NT, preferred_element_type=F32)
            old = m_scr[part]
            new = jnp.maximum(old, jnp.max(s, axis=-1, keepdims=True))
            m_scr[part] = new
            w = jnp.exp2((s - jnp.tile(new, (1, QUAD // HD))) * factor)
            alpha = jnp.exp2((old - new) * factor)
            acc_scr[part] = acc_scr[part] * jnp.tile(alpha, (1, 2)) + jnp.dot(
                w.astype(BF), values, preferred_element_type=F32)

    for g in range(8):
        part = pl.ds(g * 128, 128)
        o_ref[:, g * 128:(g + 1) * 128] = (acc_scr[part, :HD] / acc_scr[part, HD:]).astype(BF)


def attend(p, bounds, query, near, far):
    pieces = [*near, *far]
    vm = pl.BlockSpec(memory_space=pltpu.VMEM)
    return pl.pallas_call(
        functools.partial(attend_kernel, p),
        in_specs=[pl.BlockSpec(memory_space=pltpu.SMEM)] + [vm] * 9,
        out_specs=vm,
        out_shape=jax.ShapeDtypeStruct((128, 1024), BF),
        scratch_shapes=[
            pltpu.VMEM((1024, 2 * HD), BF),
            pltpu.VMEM((1024, HD), F32),
            pltpu.VMEM((1024, 2 * HD), F32),
        ],
        compiler_params=pltpu.CompilerParams(vmem_limit_bytes=32 << 20),
        cost_estimate=pl.CostEstimate(flops=4 * 10**9, bytes_accessed=3 * 10**6, transcendentals=5 * 10**6),
        name="attend",
    )(bounds, query, *pieces)


def pack_kernel(*refs):
    for n, ref in enumerate(refs[:-1]):
        refs[-1][n] = ref[...]


def pack(parts):
    vm = pl.BlockSpec(memory_space=pltpu.VMEM)
    return pl.pallas_call(
        pack_kernel,
        in_specs=[vm] * len(parts),
        out_specs=vm,
        out_shape=jax.ShapeDtypeStruct((len(parts),) + parts[0].shape, BF),
        compiler_params=pltpu.CompilerParams(vmem_limit_bytes=8 << 20),
        cost_estimate=pl.CostEstimate(flops=0, bytes_accessed=10**6, transcendentals=0),
        name="pack",
    )(*parts)


def context_part(context_query, context_key, context_value, documents):
    s = lax.axis_index("seq")
    z = s // (NX * NY)
    a = z // 2
    odd, hi = a & 1, a >> 1
    head = [
        jnp.concatenate([t[:, j * HD:(j + 1) * HD] for t in (context_key, context_value)], axis=1)
        for j in range(2)
    ]
    got = []
    for p in range(2):
        got.append(lax.ppermute(jnp.where((hi ^ p) == 0, head[0], head[1]), BOTH, quad_move(p)))
    mine = jnp.where(odd == 0, jnp.stack(got), jnp.stack(got[::-1]))
    parts = [mine]
    for d, e in ((0, 1), (1, 0), (1, 1)):
        parts.append(lax.ppermute(mine, "seq", [(t, t ^ (8 * d + 4 * e)) for t in range(64)]))
    near = [pack(parts)]
    for step in (1, -1, 2):
        near.append(lax.ppermute(near[0], "seq", [(t, t // 4 * 4 + (t + step) % 4) for t in range(64)]))
    far = []
    for n in range(4):
        far.append(lax.ppermute(near[n], "section", [(0, 1), (1, 0)]))
    queries = []
    for p in range(2):
        queries.append(lax.ppermute(
            jnp.where((hi ^ p) == 0, context_query[:, :1024], context_query[:, 1024:]),
            BOTH, quad_move(p)))
    bounds = jnp.sum(documents[None, :] < jnp.arange(16, dtype=jnp.int32)[:, None], axis=1).astype(jnp.int32)
    back = []
    for p in range(2):
        o = attend(p, bounds, queries[p], near, far)
        back.append(lax.ppermute(o, BOTH, [(t, f) for f, t in quad_move(p)]))
    return jnp.where(hi == 0, jnp.concatenate(back, axis=1), jnp.concatenate(back[::-1], axis=1))


def program(
    patches,
    inner_weight,
    norm_gain,
    outer_weight,
    merge_gain,
    windows,
    owners,
    context_query,
    context_key,
    context_value,
    documents,
):
    send, keep = vision(patches, inner_weight, norm_gain, outer_weight, windows)
    recv = lax.ppermute(send, "mp", [(0, 1), (1, 0)])
    tokens = owners.shape[0]
    target = owners[:, 0]
    order = jnp.arange(tokens, dtype=jnp.int32)
    earlier = (target[:, None] == target[None, :]) & (order[:, None] < order[None, :])
    slot = target * 2 + jnp.sum(earlier, axis=0).astype(jnp.int32)
    spot = 4 * jnp.tile(slot[None, :], (1, 4)) + jnp.arange(4 * tokens, dtype=jnp.int32)[None, :] // tokens
    owner_count = lax.axis_size(BOTH)
    outgoing = merge(keep, recv, merge_gain, spot, owner_count * 2)
    arrived = lax.all_to_all(
        outgoing.reshape(owner_count, 8, outgoing.shape[1]), BOTH, split_axis=0, concat_axis=0, tiled=True)
    delivered = place(arrived.reshape(outgoing.shape))
    attended = context_part(context_query, context_key, context_value, documents)
    return (delivered, attended)


def solution(mesh):
    in_specs = (
        P(BOTH, None),
        P(None, None, "mp"),
        P(),
        P("mp", None),
        P(),
        P(BOTH, None),
        P(BOTH, None),
        P("seq", ("section", "mp")),
        P("seq", ("section", "mp")),
        P("seq", ("section", "mp")),
        P(),
    )
    out_specs = (P(BOTH, "mp"), P("seq", ("section", "mp")))
    return jax.shard_map(program, mesh=mesh, in_specs=in_specs, out_specs=out_specs, check_vma=False)
```
